32 devices in a mesh: grp: 2 (over y), seq: 4 (over z), fsdp: 2 (over x), chan: 2 (over core).
Axes of the slice: x: 2, y: 2, z: 4, core: 2. Of those that a mesh axis runs over, the one named last changes fastest.
Arguments:
- tokens: bfloat16 [2048, 4096], P(('grp', 'seq', 'fsdp'), 'chan'), parts along dimension 0, may hold values from -6 to 6
- proj_weight: bfloat16 [4096, 3, 512], P('fsdp', None, 'chan'), may hold values from -0.09375 to 0.09375
- short_weight: float32 [3, 3, 512], P(None, None, 'chan'), may hold values from -3 to 3
- skip_gain: float32 [512], P('chan'), may hold values from -4 to 4
- filter_taps: bfloat16 [1024, 512], P(('seq', 'fsdp'), 'chan'), may hold values from -0.1875 to 0.1875
Outputs:
- mixed_out: bfloat16 [2048, 512], P(('grp', 'seq', 'fsdp'), 'chan'), parts along dimension 0
The draws below stay inside these ranges and needn't reach their ends.
There are 2 independent parts, one for each index of `grp`. The reference program is written for one: setup_inputs(seed, part) draws one part's arguments, and reference() takes and returns one part's arrays. A program takes and returns all parts, laid end to end along the dimension named above; an argument that names none is the same for every part. Nothing has to cross between parts.
All inputs are finite; a program needn't handle non-finite values.
Results may differ from the reference program's by a relative error of at most 0.009.
Values may be sent and summed in bfloat16 or wider, within the bound.
A program may use at most 64 MiB of HBM per device.

```python
import math
import jax
import jax.numpy as jnp
from jax import lax

D = 4096
C = 512
TOK_DEV = 128
L = 1024


def block_scale(rng, dims, split, low, top_value):
    factor_of = 1.0
    for dim, parts in split:
        steps = jax.random.uniform(jax.random.fold_in(jax.random.fold_in(rng, 6), dim), (parts,), jnp.float32, low / len(split), top_value / len(split))
        factor_of = factor_of * jnp.repeat(jnp.exp(steps), dims[dim] // parts).reshape((-1,) + (1,) * (len(dims) - 1 - dim))
    return factor_of


def normal_values(own_key, dims, deviation, bound, shards=(), kind=jnp.bfloat16):
    drawn = deviation * jax.random.normal(own_key, dims, jnp.float32)
    if shards:
        drawn = drawn * block_scale(own_key, dims, shards, -0.22, 0.18)
    return jnp.clip(drawn, -bound, bound).astype(kind)


def setup_inputs(seed: int = 0, part: int = 0) -> dict:
    splits = jax.random.split(jax.random.key(seed), 6)
    own_keys = jax.random.split(jax.random.fold_in(splits[5], part), 6)
    return {
        "tokens": normal_values(own_keys[0], (L, D), 1.0, 6.0, ((0, 8), (1, 2))),
        "proj_weight": normal_values(splits[1], (D, 3, C), D ** -0.5, 0.09375, ((0, 2), (2, 2))),
        "short_weight": normal_values(splits[2], (3, 3, C), 0.6, 3.0, ((2, 2),), jnp.float32),
        "skip_gain": normal_values(splits[3], (C,), 1.0, 4.0, ((0, 2),), jnp.float32),
        "filter_taps": normal_values(splits[4], (L, C), L ** -0.5, 0.1875, ((0, 8), (1, 2))),
    }


highest = lax.Precision.HIGHEST


def rounded(value):
    return lax.optimization_barrier(value.astype(jnp.bfloat16))


def index_grid(row_count, col_count):
    return (lax.broadcasted_iota(jnp.int32, (row_count, col_count), 0),
            lax.broadcasted_iota(jnp.int32, (row_count, col_count), 1))


def phase_pair(row_ids, col_ids, period):
    wrapped = (row_ids * col_ids) % period
    phase = wrapped.astype(jnp.float32) * (2.0 * math.pi / period)
    return jnp.cos(phase), jnp.sin(phase)


def spectrum(signal, first_cos, first_sin, twist_cos, twist_sin, last_cos, last_sin):
    values = signal.astype(jnp.float32)
    real_a = jnp.einsum("qp,bpm->bqm", first_cos, values, precision=highest)
    imag_a = -jnp.einsum("qp,bpm->bqm", first_sin, values, precision=highest)
    real_b = rounded(real_a * twist_cos + imag_a * twist_sin).astype(jnp.float32)
    imag_b = rounded(imag_a * twist_cos - real_a * twist_sin).astype(jnp.float32)
    real_x = jnp.einsum("bqm,mr->bqr", real_b, last_cos, precision=highest) + jnp.einsum("bqm,mr->bqr", imag_b, last_sin, precision=highest)
    imag_x = jnp.einsum("bqm,mr->bqr", imag_b, last_cos, precision=highest) - jnp.einsum("bqm,mr->bqr", real_b, last_sin, precision=highest)
    return rounded(real_x).astype(jnp.float32), rounded(imag_x).astype(jnp.float32)


def invert(real_z, imag_z, first_cos, first_sin, twist_cos, twist_sin, last_cos, last_sin, length):
    real_v = jnp.einsum("bqr,mr->bqm", real_z, last_cos, precision=highest) - jnp.einsum("bqr,mr->bqm", imag_z, last_sin, precision=highest)
    imag_v = jnp.einsum("bqr,mr->bqm", imag_z, last_cos, precision=highest) + jnp.einsum("bqr,mr->bqm", real_z, last_sin, precision=highest)
    real_w = rounded(real_v * twist_cos - imag_v * twist_sin).astype(jnp.float32)
    imag_w = rounded(imag_v * twist_cos + real_v * twist_sin).astype(jnp.float32)
    summed = jnp.einsum("qp,bqm->bpm", first_cos, real_w, precision=highest) - jnp.einsum("qp,bqm->bpm", first_sin, imag_w, precision=highest)
    return (summed * (1.0 / length)).astype(jnp.bfloat16)


def reference(tokens, proj_weight, short_weight, skip_gain, filter_taps):
    total_rows, model_width = tokens.shape
    width = proj_weight.shape[2]
    block_rows = TOK_DEV
    weight_flat = proj_weight.reshape(model_width, 3 * width).astype(jnp.float32)

    def project(block):
        return jnp.dot(block.astype(jnp.float32), weight_flat, precision=highest).astype(jnp.bfloat16)

    projected = lax.map(project, tokens.reshape(total_rows // block_rows, block_rows, model_width))
    projected = lax.optimization_barrier(projected)
    projected = projected.reshape(total_rows, 3, width).astype(jnp.float32)
    padded = jnp.pad(projected, ((2, 0), (0, 0), (0, 0)))
    mixed = short_weight[0] * padded[2:] + short_weight[1] * padded[1:-1] + short_weight[2] * padded[:-2]
    query = mixed[:, 0]
    product = rounded(mixed[:, 1] * mixed[:, 2])

    half_rows = total_rows // block_rows
    period_rows = 2 * half_rows
    length = period_rows * block_rows
    bin_ids, tap_ids = index_grid(period_rows, half_rows)
    first_cos, first_sin = phase_pair(bin_ids, tap_ids, period_rows)
    first_cos = rounded(first_cos).astype(jnp.float32)
    first_sin = rounded(first_sin).astype(jnp.float32)
    col_ids, freq_ids = index_grid(block_rows, block_rows)
    last_cos, last_sin = phase_pair(col_ids, freq_ids, block_rows)
    last_cos = rounded(last_cos).astype(jnp.float32)
    last_sin = rounded(last_sin).astype(jnp.float32)
    row_ids, mid_ids = index_grid(period_rows, block_rows)
    twist_cos, twist_sin = phase_pair(row_ids, mid_ids, length)

    group_size = 8
    signal_blocks = jnp.transpose(product).reshape(width // group_size, group_size, half_rows, block_rows)
    filter_blocks = jnp.transpose(filter_taps).reshape(width // group_size, group_size, half_rows, block_rows)

    def convolve(pair):
        signal, taps = pair
        sig_real, sig_imag = spectrum(signal, first_cos, first_sin, twist_cos, twist_sin, last_cos, last_sin)
        tap_real, tap_imag = spectrum(taps, first_cos, first_sin, twist_cos, twist_sin, last_cos, last_sin)
        real_z = rounded(sig_real * tap_real - sig_imag * tap_imag).astype(jnp.float32)
        imag_z = rounded(sig_real * tap_imag + sig_imag * tap_real).astype(jnp.float32)
        return invert(real_z, imag_z, first_cos, first_sin, twist_cos, twist_sin, last_cos, last_sin, length)

    convolved = lax.map(convolve, (signal_blocks, filter_blocks))
    conv = jnp.transpose(convolved.reshape(width, total_rows))
    result = query * (conv.astype(jnp.float32) + skip_gain * product.astype(jnp.float32))
    return result.astype(jnp.bfloat16)
```

```python
import functools
import math

import jax
import jax.numpy as jnp
import ml_dtypes
import numpy as np
from jax import lax
from jax.experimental import pallas as pl
from jax.experimental.pallas import tpu as pltpu
from jax.sharding import PartitionSpec as P

MESH = pl.DeviceIdType.MESH
BF16 = jnp.bfloat16
F32 = jnp.float32
CHUNKS = 4


def phase_pair(rows, cols, period):
    wrapped = (np.arange(rows)[:, None] * np.arange(cols)[None, :]) % period
    phase = wrapped.astype(np.float32) * np.float32(2.0 * math.pi / period)
    return np.cos(phase), np.sin(phase)


def tables(groups, per, rows):
    bf = ml_dtypes.bfloat16
    bins = 2 * groups
    cos, sin = phase_pair(bins, groups, bins)
    eye = np.eye(per, dtype=np.float32)
    first = np.concatenate([np.kron(cos, eye), np.kron(-sin, eye)], axis=0).astype(bf)
    cos, sin = phase_pair(rows, rows, rows)
    ahead = np.block([[cos, -sin], [sin, cos]]).astype(bf)
    behind = np.block([[cos, sin], [-sin, cos]]).astype(bf)
    cos, sin = phase_pair(bins, rows, bins * rows)
    twist = np.stack([np.repeat(cos, per, axis=0), np.repeat(sin, per, axis=0)])
    last = np.ascontiguousarray(first.T)
    return first, last, ahead, behind, twist.astype(np.float32)


def kernel(
    sizes,
    tokens,
    weight,
    short,
    gain,
    taps,
    first_h,
    last_h,
    ahead_h,
    behind_h,
    twist_h,
    out,
    w,
    first,
    last,
    ahead,
    behind,
    twist,
    held,
    acc,
    psend,
    precv,
    hsend,
    hrecv,
    query,
    product,
    tsend,
    trecv,
    gsend,
    grecv,
    csend,
    crecv,
    tapspec,
    load_sem,
    tok_send,
    tok_recv,
    part_send,
    part_recv,
    halo_sem,
    a2a_send,
    a2a_recv,
):
    seq, fsdp, chan = sizes
    groups = seq * fsdp
    rows = tokens.shape[0]
    depth = weight.shape[1]
    width = weight.shape[2]
    per = width // groups
    bins = 2 * groups
    step = depth // CHUNKS
    share = fsdp // chan
    s = lax.axis_index("seq")
    f = lax.axis_index("fsdp")
    c = lax.axis_index("chan")
    me = s * fsdp + f

    loads = [
        pltpu.make_async_copy(source, target, load_sem.at[i])
        for i, (source, target) in enumerate(
            [
                (weight, w),
                (first_h, first),
                (last_h, last),
                (ahead_h, ahead),
                (behind_h, behind),
                (twist_h, twist),
            ]
        )
    ]
    for load in loads:
        load.start()

    barrier = pltpu.get_barrier_semaphore()
    everyone = groups * chan

    def greet(k, carry):
        other = lax.rem(me * chan + c + k, everyone)
        spot = other // chan
        pl.semaphore_signal(
            barrier,
            inc=1,
            device_id={"seq": spot // fsdp, "fsdp": spot % fsdp, "chan": other % chan},
            device_id_type=MESH,
        )
        return carry

    lax.fori_loop(1, everyone, greet, 0)
    pl.semaphore_wait(barrier, everyone - 1)

    def token_copy(i, cc, k):
        return pltpu.make_async_remote_copy(
            src_ref=tokens.at[:, pl.ds(i * depth + k * step, step)],
            dst_ref=held.at[f, k],
            send_sem=tok_send.at[i * chan + cc, k],
            recv_sem=tok_recv.at[f, k],
            device_id={"fsdp": c * share + i, "chan": cc},
            device_id_type=MESH,
        )

    def own_copy(i, k):
        return pltpu.make_async_copy(
            tokens.at[:, pl.ds(i * depth + k * step, step)], held.at[f, k], tok_recv.at[f, k]
        )

    for k in range(CHUNKS):
        for i in range(share):
            for cc in range(chan):
                is_self = jnp.logical_and(c * share + i == f, c == cc)

                @pl.when(jnp.logical_not(is_self))
                def _():
                    token_copy(i, cc, k).start()

                @pl.when(is_self)
                def _():
                    own_copy(i, k).start()

    def exchange_copy(which, source, target, k):
        other = lax.rem(me + k, groups)
        return pltpu.make_async_remote_copy(
            src_ref=source.at[other],
            dst_ref=target.at[me],
            send_sem=a2a_send.at[which, k],
            recv_sem=a2a_recv.at[which, k],
            device_id={"seq": other // fsdp, "fsdp": other % fsdp},
            device_id_type=MESH,
        )

    def exchange_start(which, source, target):
        def go(k, carry):
            exchange_copy(which, source, target, k).start()
            return carry

        lax.fori_loop(1, groups, go, 0)
        target[me] = source[me]

    def exchange_wait(which, source, target):
        def go(k, carry):
            copy = exchange_copy(which, source, target, k)
            copy.wait_send()
            copy.wait_recv()
            return carry

        lax.fori_loop(1, groups, go, 0)

    tsend[...] = jnp.transpose(taps[...].astype(F32)).astype(BF16).reshape(groups, per, rows)
    exchange_start(0, tsend, trecv)

    half = bins * per

    def spectrum(signal):
        a = jnp.dot(first[...], signal, preferred_element_type=F32)
        real_a, imag_a = a[:half], a[half:]
        real_b = (real_a * twist[0] + imag_a * twist[1]).astype(BF16)
        imag_b = (imag_a * twist[0] - real_a * twist[1]).astype(BF16)
        b = jnp.concatenate([real_b, imag_b], axis=1)
        return jnp.dot(b, ahead[...], preferred_element_type=F32).astype(BF16)

    for load in loads[1:]:
        load.wait()
    exchange_wait(0, tsend, trecv)
    tapspec[...] = spectrum(trecv[...].reshape(width, rows))
    loads[0].wait()

    def part_copy(d):
        other = lax.rem(f + d, fsdp)
        return pltpu.make_async_remote_copy(
            src_ref=psend.at[d - 1],
            dst_ref=precv.at[d - 1],
            send_sem=part_send.at[d - 1],
            recv_sem=part_recv.at[d - 1],
            device_id={"fsdp": other},
            device_id_type=MESH,
        )

    for d in range(1, fsdp + 1):
        spot = lax.rem(f + d, fsdp)
        for k in range(CHUNKS):
            pltpu.make_async_copy(held.at[spot, k], held.at[spot, k], tok_recv.at[spot, k]).wait()
            block = held[spot, k]
            for j in range(3):
                term = jnp.dot(
                    block, w[j, k * step : (k + 1) * step, :], preferred_element_type=F32
                )
                if k == 0:
                    acc[j] = term
                else:
                    acc[j] += term
        if d < fsdp:
            psend[d - 1] = acc[...].astype(BF16)
            part_copy(d).start()

    for d in range(1, fsdp):
        part_copy(d).wait_recv()
    total = acc[...]
    for d in range(1, fsdp):
        total = total + precv[d - 1].astype(F32)
    projected = total.astype(BF16).astype(F32)

    following = jnp.minimum(me + 1, groups - 1)
    halo = pltpu.make_async_remote_copy(
        src_ref=hsend,
        dst_ref=hrecv,
        send_sem=halo_sem.at[0],
        recv_sem=halo_sem.at[1],
        device_id={"seq": following // fsdp, "fsdp": following % fsdp},
        device_id_type=MESH,
    )
    hsend[...] = projected[:, rows - 8 :, :]

    @pl.when(me < groups - 1)
    def _():
        halo.start()

    @pl.when(me == 0)
    def _():
        hrecv[...] = jnp.zeros_like(hrecv)

    @pl.when(me > 0)
    def _():
        halo.wait_recv()

    row_ids = lax.broadcasted_iota(jnp.int32, (rows, width), 0)
    branches = []
    for j in range(3):
        now = projected[j]
        before = hrecv[j, 7:8, :]
        earlier = hrecv[j, 6:7, :]
        one = jnp.where(row_ids == 0, before, pltpu.roll(now, 1, 0))
        two = jnp.where(
            row_ids == 0, earlier, jnp.where(row_ids == 1, before, pltpu.roll(now, 2, 0))
        )
        branches.append(
            short[0, j : j + 1, :] * now
            + short[1, j : j + 1, :] * one
            + short[2, j : j + 1, :] * two
        )
    prod = (branches[1] * branches[2]).astype(BF16).astype(F32)
    gsend[...] = jnp.transpose(prod).astype(BF16).reshape(groups, per, rows)
    exchange_start(1, gsend, grecv)
    query[...] = branches[0]
    product[...] = prod * gain[...]
    exchange_wait(1, gsend, grecv)

    x = spectrum(grecv[...].reshape(width, rows)).astype(F32)
    t = tapspec[...].astype(F32)
    xr, xi = x[:, :rows], x[:, rows:]
    tr, ti = t[:, :rows], t[:, rows:]
    real_z = (xr * tr - xi * ti).astype(BF16)
    imag_z = (xr * ti + xi * tr).astype(BF16)
    z = jnp.concatenate([real_z, imag_z], axis=1)
    v = jnp.dot(z, behind[...], preferred_element_type=F32)
    vr, vi = v[:, :rows], v[:, rows:]
    real_w = (vr * twist[0] - vi * twist[1]).astype(BF16)
    imag_w = (vi * twist[0] + vr * twist[1]).astype(BF16)
    packed = jnp.concatenate([real_w, imag_w], axis=0)
    y = jnp.dot(last[...], packed, preferred_element_type=F32) * (1.0 / (bins * rows))
    csend[...] = y.astype(BF16).reshape(groups, per, rows)
    exchange_start(2, csend, crecv)
    exchange_wait(2, csend, crecv)
    conv = jnp.transpose(crecv[...].reshape(width, rows).astype(F32))
    out[...] = (query[...] * (conv + product[...])).astype(BF16)

    @pl.when(me < groups - 1)
    def _():
        halo.wait_send()

    for d in range(1, fsdp):
        part_copy(d).wait_send()
    for k in range(CHUNKS):
        for i in range(share):
            for cc in range(chan):
                is_self = jnp.logical_and(c * share + i == f, c == cc)

                @pl.when(jnp.logical_not(is_self))
                def _():
                    token_copy(i, cc, k).wait_send()


def per_device(sizes, tokens, proj_weight, short_weight, skip_gain, filter_taps):
    seq, fsdp, chan = sizes
    groups = seq * fsdp
    rows = tokens.shape[0]
    depth, branches, width = proj_weight.shape
    per = width // groups
    made = tables(groups, per, rows)
    dma = pltpu.SemaphoreType.DMA
    vmem = pl.BlockSpec(memory_space=pltpu.VMEM)
    anywhere = pl.BlockSpec(memory_space=pl.ANY)
    half = 2 * groups * per
    return pl.pallas_call(
        functools.partial(kernel, sizes),
        out_shape=jax.ShapeDtypeStruct((rows, width), BF16),
        in_specs=[anywhere, anywhere, vmem, vmem, vmem] + [anywhere] * 5,
        out_specs=vmem,
        scratch_shapes=[
            pltpu.VMEM((branches, depth, width), BF16),
            pltpu.VMEM(made[0].shape, BF16),
            pltpu.VMEM(made[1].shape, BF16),
            pltpu.VMEM(made[2].shape, BF16),
            pltpu.VMEM(made[3].shape, BF16),
            pltpu.VMEM(made[4].shape, F32),
            pltpu.VMEM((fsdp, CHUNKS, rows, depth // CHUNKS), BF16),
            pltpu.VMEM((branches, rows, width), F32),
            pltpu.VMEM((fsdp - 1, branches, rows, width), BF16),
            pltpu.VMEM((fsdp - 1, branches, rows, width), BF16),
            pltpu.VMEM((branches, 8, width), F32),
            pltpu.VMEM((branches, 8, width), F32),
            pltpu.VMEM((rows, width), F32),
            pltpu.VMEM((rows, width), F32),
        ]
        + [pltpu.VMEM((groups, per, rows), BF16)] * 6
        + [
            pltpu.VMEM((half, 2 * rows), BF16),
            dma((6,)),
            dma((fsdp, CHUNKS)),
            dma((fsdp, CHUNKS)),
            dma((fsdp - 1,)),
            dma((fsdp - 1,)),
            dma((2,)),
            dma((3, groups)),
            dma((3, groups)),
        ],
        compiler_params=pltpu.CompilerParams(
            collective_id=0, has_side_effects=True, vmem_limit_bytes=48 * 1024 * 1024
        ),
        name="hyena",
    )(
        tokens,
        jnp.transpose(proj_weight, (1, 0, 2)),
        short_weight,
        skip_gain.reshape(1, width),
        filter_taps,
        *[jnp.asarray(table) for table in made],
    )


def solution(mesh):
    sizes = (mesh.shape["seq"], mesh.shape["fsdp"], mesh.shape["chan"])
    in_specs = (
        P(("grp", "seq", "fsdp"), "chan"),
        P("fsdp", None, "chan"),
        P(None, None, "chan"),
        P("chan"),
        P(("seq", "fsdp"), "chan"),
    )
    out_specs = P(("grp", "seq", "fsdp"), "chan")
    return jax.shard_map(
        functools.partial(per_device, sizes),
        mesh=mesh,
        in_specs=in_specs,
        out_specs=out_specs,
        check_vma=False,
    )
```

```python
import functools
import math

import jax
import jax.numpy as jnp
import ml_dtypes
import numpy as np
from jax import lax
from jax.experimental import pallas as pl
from jax.experimental.pallas import tpu as pltpu
from jax.sharding import PartitionSpec as P

MESH = pl.DeviceIdType.MESH
BF16 = jnp.bfloat16
F32 = jnp.float32
CHUNKS = 4


def phase_pair(rows, cols, period):
    wrapped = (np.arange(rows)[:, None] * np.arange(cols)[None, :]) % period
    phase = wrapped.astype(np.float32) * np.float32(2.0 * math.pi / period)
    return np.cos(phase), np.sin(phase)


def tables(groups, per, rows):
    bf = ml_dtypes.bfloat16
    bins = 2 * groups
    cos, sin = phase_pair(bins, groups, bins)
    eye = np.eye(per, dtype=np.float32)
    first = np.concatenate([np.kron(cos, eye), np.kron(-sin, eye)], axis=0).astype(bf)
    cos, sin = phase_pair(rows, rows, rows)
    ahead = np.block([[cos, -sin], [sin, cos]]).astype(bf)
    behind = np.block([[cos, sin], [-sin, cos]]).astype(bf)
    cos, sin = phase_pair(bins, rows, bins * rows)
    twist = np.stack([np.repeat(cos, per, axis=0), np.repeat(sin, per, axis=0)])
    last = np.ascontiguousarray(first.T)
    return first, last, ahead, behind, twist.astype(np.float32)


def kernel(
    sizes,
    tokens,
    weight,
    short_h,
    gain_h,
    taps_h,
    first_h,
    last_h,
    ahead_h,
    behind_h,
    twist_h,
    out,
    w,
    first,
    last,
    ahead,
    behind,
    twist,
    short,
    gain,
    taps,
    held,
    acc,
    psend,
    precv,
    hsend,
    hrecv,
    query,
    product,
    tsend,
    trecv,
    gsend,
    grecv,
    csend,
    crecv,
    tapspec,
    load_sem,
    tok_send,
    tok_recv,
    part_send,
    part_recv,
    halo_sem,
    a2a_send,
    a2a_recv,
):
    seq, fsdp, chan = sizes
    groups = seq * fsdp
    rows = tokens.shape[0]
    depth = weight.shape[1]
    width = weight.shape[2]
    per = width // groups
    bins = 2 * groups
    step = depth // CHUNKS
    share = fsdp // chan
    s = lax.axis_index("seq")
    f = lax.axis_index("fsdp")
    c = lax.axis_index("chan")
    me = s * fsdp + f

    loads = [
        pltpu.make_async_copy(source, target, load_sem.at[i])
        for i, (source, target) in enumerate(
            [
                (taps_h, taps),
                (weight, w),
                (first_h, first),
                (ahead_h, ahead),
                (twist_h, twist),
                (last_h, last),
                (behind_h, behind),
                (short_h, short),
                (gain_h, gain),
            ]
        )
    ]
    for load in loads:
        load.start()

    barrier = pltpu.get_barrier_semaphore()
    everyone = groups * chan

    def greet(k, carry):
        other = lax.rem(me * chan + c + k, everyone)
        spot = other // chan
        pl.semaphore_signal(
            barrier,
            inc=1,
            device_id={"seq": spot // fsdp, "fsdp": spot % fsdp, "chan": other % chan},
            device_id_type=MESH,
        )
        return carry

    lax.fori_loop(1, everyone, greet, 0)
    pl.semaphore_wait(barrier, everyone - 1)

    def token_copy(i, cc, k):
        return pltpu.make_async_remote_copy(
            src_ref=tokens.at[:, pl.ds(i * depth + k * step, step)],
            dst_ref=held.at[f, k],
            send_sem=tok_send.at[i * chan + cc, k],
            recv_sem=tok_recv.at[f, k],
            device_id={"fsdp": c * share + i, "chan": cc},
            device_id_type=MESH,
        )

    def own_copy(i, k):
        return pltpu.make_async_copy(
            tokens.at[:, pl.ds(i * depth + k * step, step)], held.at[f, k], tok_recv.at[f, k]
        )

    for k in range(CHUNKS):
        for i in range(share):
            for cc in range(chan):
                is_self = jnp.logical_and(c * share + i == f, c == cc)

                @pl.when(jnp.logical_not(is_self))
                def _():
                    token_copy(i, cc, k).start()

                @pl.when(is_self)
                def _():
                    own_copy(i, k).start()

    def exchange_copy(which, source, target, k):
        other = lax.rem(me + k, groups)
        return pltpu.make_async_remote_copy(
            src_ref=source.at[other],
            dst_ref=target.at[me],
            send_sem=a2a_send.at[which, k],
            recv_sem=a2a_recv.at[which, k],
            device_id={"seq": other // fsdp, "fsdp": other % fsdp},
            device_id_type=MESH,
        )

    def exchange_start(which, source, target):
        def go(k, carry):
            exchange_copy(which, source, target, k).start()
            return carry

        lax.fori_loop(1, groups, go, 0)
        target[me] = source[me]

    def exchange_wait(which, source, target):
        def go(k, carry):
            copy = exchange_copy(which, source, target, k)
            copy.wait_send()
            copy.wait_recv()
            return carry

        lax.fori_loop(1, groups, go, 0)

    loads[0].wait()
    tsend[...] = jnp.transpose(taps[...].astype(F32)).astype(BF16).reshape(groups, per, rows)
    exchange_start(0, tsend, trecv)

    half = bins * per

    def spectrum(signal):
        a = jnp.dot(first[...], signal, preferred_element_type=F32)
        real_a, imag_a = a[:half], a[half:]
        real_b = (real_a * twist[0] + imag_a * twist[1]).astype(BF16)
        imag_b = (imag_a * twist[0] - real_a * twist[1]).astype(BF16)
        b = jnp.concatenate([real_b, imag_b], axis=1)
        return jnp.dot(b, ahead[...], preferred_element_type=F32).astype(BF16)

    for load in loads[1:]:
        load.wait()
    exchange_wait(0, tsend, trecv)
    tapspec[...] = spectrum(trecv[...].reshape(width, rows))

    def part_copy(d):
        other = lax.rem(f + d, fsdp)
        return pltpu.make_async_remote_copy(
            src_ref=psend.at[d - 1],
            dst_ref=precv.at[d - 1],
            send_sem=part_send.at[d - 1],
            recv_sem=part_recv.at[d - 1],
            device_id={"fsdp": other},
            device_id_type=MESH,
        )

    for d in range(1, fsdp + 1):
        spot = lax.rem(f + d, fsdp)
        for k in range(CHUNKS):
            pltpu.make_async_copy(held.at[spot, k], held.at[spot, k], tok_recv.at[spot, k]).wait()
            block = held[spot, k]
            for j in range(3):
                term = jnp.dot(
                    block, w[j, k * step : (k + 1) * step, :], preferred_element_type=F32
                )
                if k == 0:
                    acc[j] = term
                else:
                    acc[j] += term
        if d < fsdp:
            psend[d - 1] = acc[...].astype(BF16)
            part_copy(d).start()

    for d in range(1, fsdp):
        part_copy(d).wait_recv()
    total = acc[...]
    for d in range(1, fsdp):
        total = total + precv[d - 1].astype(F32)
    projected = total.astype(BF16).astype(F32)

    following = jnp.minimum(me + 1, groups - 1)
    halo = pltpu.make_async_remote_copy(
        src_ref=hsend,
        dst_ref=hrecv,
        send_sem=halo_sem.at[0],
        recv_sem=halo_sem.at[1],
        device_id={"seq": following // fsdp, "fsdp": following % fsdp},
        device_id_type=MESH,
    )
    hsend[...] = projected[:, rows - 8 :, :]

    @pl.when(me < groups - 1)
    def _():
        halo.start()

    @pl.when(me == 0)
    def _():
        hrecv[...] = jnp.zeros_like(hrecv)

    @pl.when(me > 0)
    def _():
        halo.wait_recv()

    row_ids = lax.broadcasted_iota(jnp.int32, (rows, width), 0)
    branches = []
    for j in range(3):
        now = projected[j]
        before = hrecv[j, 7:8, :]
        earlier = hrecv[j, 6:7, :]
        one = jnp.where(row_ids == 0, before, pltpu.roll(now, 1, 0))
        two = jnp.where(
            row_ids == 0, earlier, jnp.where(row_ids == 1, before, pltpu.roll(now, 2, 0))
        )
        branches.append(
            short[0, j : j + 1, :] * now
            + short[1, j : j + 1, :] * one
            + short[2, j : j + 1, :] * two
        )
    prod = (branches[1] * branches[2]).astype(BF16).astype(F32)
    gsend[...] = jnp.transpose(prod).astype(BF16).reshape(groups, per, rows)
    exchange_start(1, gsend, grecv)
    query[...] = branches[0]
    product[...] = prod * gain[...]
    exchange_wait(1, gsend, grecv)

    x = spectrum(grecv[...].reshape(width, rows)).astype(F32)
    t = tapspec[...].astype(F32)
    xr, xi = x[:, :rows], x[:, rows:]
    tr, ti = t[:, :rows], t[:, rows:]
    real_z = (xr * tr - xi * ti).astype(BF16)
    imag_z = (xr * ti + xi * tr).astype(BF16)
    z = jnp.concatenate([real_z, imag_z], axis=1)
    v = jnp.dot(z, behind[...], preferred_element_type=F32)
    vr, vi = v[:, :rows], v[:, rows:]
    real_w = (vr * twist[0] - vi * twist[1]).astype(BF16)
    imag_w = (vi * twist[0] + vr * twist[1]).astype(BF16)
    packed = jnp.concatenate([real_w, imag_w], axis=0)
    y = jnp.dot(last[...], packed, preferred_element_type=F32) * (1.0 / (bins * rows))
    csend[...] = y.astype(BF16).reshape(groups, per, rows)
    exchange_start(2, csend, crecv)
    exchange_wait(2, csend, crecv)
    conv = jnp.transpose(crecv[...].reshape(width, rows).astype(F32))
    out[...] = (query[...] * (conv + product[...])).astype(BF16)

    @pl.when(me < groups - 1)
    def _():
        halo.wait_send()

    for d in range(1, fsdp):
        part_copy(d).wait_send()
    for k in range(CHUNKS):
        for i in range(share):
            for cc in range(chan):
                is_self = jnp.logical_and(c * share + i == f, c == cc)

                @pl.when(jnp.logical_not(is_self))
                def _():
                    token_copy(i, cc, k).wait_send()


def per_device(sizes, tokens, proj_weight, short_weight, skip_gain, filter_taps):
    seq, fsdp, chan = sizes
    groups = seq * fsdp
    rows = tokens.shape[0]
    depth, branches, width = proj_weight.shape
    per = width // groups
    made = tables(groups, per, rows)
    dma = pltpu.SemaphoreType.DMA
    vmem = pl.BlockSpec(memory_space=pltpu.VMEM)
    hbm = pl.BlockSpec(memory_space=pl.ANY)
    half = 2 * groups * per
    return pl.pallas_call(
        functools.partial(kernel, sizes),
        out_shape=jax.ShapeDtypeStruct((rows, width), BF16),
        in_specs=[hbm] * 10,
        out_specs=vmem,
        scratch_shapes=[
            pltpu.VMEM((branches, depth, width), BF16),
            pltpu.VMEM(made[0].shape, BF16),
            pltpu.VMEM(made[1].shape, BF16),
            pltpu.VMEM(made[2].shape, BF16),
            pltpu.VMEM(made[3].shape, BF16),
            pltpu.VMEM(made[4].shape, F32),
            pltpu.VMEM(short_weight.shape, F32),
            pltpu.VMEM((1, width), F32),
            pltpu.VMEM((rows, width), BF16),
            pltpu.VMEM((fsdp, CHUNKS, rows, depth // CHUNKS), BF16),
            pltpu.VMEM((branches, rows, width), F32),
            pltpu.VMEM((fsdp - 1, branches, rows, width), BF16),
            pltpu.VMEM((fsdp - 1, branches, rows, width), BF16),
            pltpu.VMEM((branches, 8, width), F32),
            pltpu.VMEM((branches, 8, width), F32),
            pltpu.VMEM((rows, width), F32),
            pltpu.VMEM((rows, width), F32),
        ]
        + [pltpu.VMEM((groups, per, rows), BF16)] * 6
        + [
            pltpu.VMEM((half, 2 * rows), BF16),
            dma((9,)),
            dma((fsdp, CHUNKS)),
            dma((fsdp, CHUNKS)),
            dma((fsdp - 1,)),
            dma((fsdp - 1,)),
            dma((2,)),
            dma((3, groups)),
            dma((3, groups)),
        ],
        compiler_params=pltpu.CompilerParams(
            collective_id=0, has_side_effects=True, vmem_limit_bytes=60 * 1024 * 1024
        ),
        name="hyena",
    )(
        tokens,
        jnp.transpose(proj_weight, (1, 0, 2)),
        short_weight,
        skip_gain.reshape(1, width),
        filter_taps,
        *[jnp.asarray(table) for table in made],
    )


def solution(mesh):
    sizes = (mesh.shape["seq"], mesh.shape["fsdp"], mesh.shape["chan"])
    in_specs = (
        P(("grp", "seq", "fsdp"), "chan"),
        P("fsdp", None, "chan"),
        P(None, None, "chan"),
        P("chan"),
        P(("seq", "fsdp"), "chan"),
    )
    out_specs = P(("grp", "seq", "fsdp"), "chan")
    return jax.shard_map(
        functools.partial(per_device, sizes),
        mesh=mesh,
        in_specs=in_specs,
        out_specs=out_specs,
        check_vma=False,
    )
```

```python
import functools
import math

import jax
import jax.numpy as jnp
import ml_dtypes
import numpy as np
from jax import lax
from jax.experimental import pallas as pl
from jax.experimental.pallas import tpu as pltpu
from jax.sharding import PartitionSpec as P

MESH = pl.DeviceIdType.MESH
BF16 = jnp.bfloat16
F32 = jnp.float32
CHUNKS = 4


def phase_pair(rows, cols, period):
    wrapped = (np.arange(rows)[:, None] * np.arange(cols)[None, :]) % period
    phase = wrapped.astype(np.float32) * np.float32(2.0 * math.pi / period)
    return np.cos(phase), np.sin(phase)


def tables(groups, per, rows):
    bf = ml_dtypes.bfloat16
    bins = 2 * groups
    cos, sin = phase_pair(bins, groups, bins)
    eye = np.eye(per, dtype=np.float32)
    first = np.concatenate([np.kron(cos, eye), np.kron(-sin, eye)], axis=0).astype(bf)
    cos, sin = phase_pair(rows, rows, rows)
    ahead = np.block([[cos, -sin], [sin, cos]]).astype(bf)
    behind = np.block([[cos, sin], [-sin, cos]]).astype(bf)
    cos, sin = phase_pair(bins, rows, bins * rows)
    twist = np.stack([np.repeat(cos, per, axis=0), np.repeat(sin, per, axis=0)])
    last = np.ascontiguousarray(first.T)
    return first, last, ahead, behind, twist.astype(np.float32)


def kernel(
    sizes,
    tokens,
    weight,
    short_h,
    gain_h,
    taps_h,
    first_h,
    last_h,
    ahead_h,
    behind_h,
    twist_h,
    out,
    w,
    first,
    last,
    ahead,
    behind,
    twist,
    short,
    gain,
    taps,
    held,
    acc,
    psend,
    precv,
    hrecv,
    query,
    product,
    tsend,
    trecv,
    gsend,
    grecv,
    csend,
    crecv,
    tapspec,
    load_sem,
    tok_send,
    tok_recv,
    fwd_send,
    part_send,
    part_recv,
    halo_send,
    halo_recv,
    a2a_send,
    a2a_recv,
):
    seq, fsdp, chan = sizes
    groups = seq * fsdp
    rows = tokens.shape[0]
    depth = weight.shape[1] * weight.shape[2]
    width = weight.shape[3]
    per = width // groups
    bins = 2 * groups
    step = depth // CHUNKS
    share = fsdp // chan
    s = lax.axis_index("seq")
    f = lax.axis_index("fsdp")
    c = lax.axis_index("chan")
    me = s * fsdp + f

    loads = [
        pltpu.make_async_copy(source, target, load_sem.at[i])
        for i, (source, target) in enumerate(
            [
                (taps_h, taps),
                (weight.at[pl.ds(1, 2)], w.at[pl.ds(1, 2)]),
                (first_h, first),
                (ahead_h, ahead),
                (twist_h, twist),
                (last_h, last),
                (behind_h, behind),
                (short_h, short),
                (gain_h, gain),
                (weight.at[pl.ds(0, 1)], w.at[pl.ds(0, 1)]),
            ]
        )
    ]
    for load in loads:
        load.start()

    barrier = pltpu.get_barrier_semaphore()
    everyone = groups * chan

    def greet(k, carry):
        other = lax.rem(me * chan + c + k, everyone)
        spot = other // chan
        pl.semaphore_signal(
            barrier,
            inc=1,
            device_id={"seq": spot // fsdp, "fsdp": spot % fsdp, "chan": other % chan},
            device_id_type=MESH,
        )
        return carry

    lax.fori_loop(1, everyone, greet, 0)
    pl.semaphore_wait(barrier, everyone - 1)

    sibling = lax.rem(c + 1, chan)

    def token_copy(i, k, same):
        return pltpu.make_async_remote_copy(
            src_ref=tokens.at[:, pl.ds(i * depth + k * step, step)],
            dst_ref=held.at[f, k],
            send_sem=tok_send.at[i, k],
            recv_sem=tok_recv.at[f, k],
            device_id={"fsdp": c * share + i, "chan": sibling if same else k % chan},
            device_id_type=MESH,
        )

    for k in range(CHUNKS):
        for i in range(share):
            stays = c * share + i == f

            @pl.when(jnp.logical_not(stays))
            def _():
                token_copy(i, k, False).start()

            @pl.when(stays)
            def _():
                token_copy(i, k, True).start()
                pltpu.make_async_copy(
                    tokens.at[:, pl.ds(i * depth + k * step, step)],
                    held.at[f, k],
                    tok_recv.at[f, k],
                ).start()

    def exchange_copy(which, source, target, k):
        other = lax.rem(me + k, groups)
        return pltpu.make_async_remote_copy(
            src_ref=source.at[other],
            dst_ref=target.at[me],
            send_sem=a2a_send.at[which, k],
            recv_sem=a2a_recv.at[which, k],
            device_id={"seq": other // fsdp, "fsdp": other % fsdp},
            device_id_type=MESH,
        )

    def exchange_start(which, source, target):
        def go(k, carry):
            exchange_copy(which, source, target, k).start()
            return carry

        lax.fori_loop(1, groups, go, 0)
        target[me] = source[me]

    def exchange_wait(which, source, target):
        def go(k, carry):
            copy = exchange_copy(which, source, target, k)
            copy.wait_send()
            copy.wait_recv()
            return carry

        lax.fori_loop(1, groups, go, 0)

    loads[0].wait()
    tsend[...] = jnp.transpose(taps[...].astype(F32)).astype(BF16).reshape(groups, per, rows)
    exchange_start(0, tsend, trecv)

    half = bins * per

    def spectrum(signal):
        a = jnp.dot(first[...], signal, preferred_element_type=F32)
        real_a, imag_a = a[:half], a[half:]
        real_b = (real_a * twist[0] + imag_a * twist[1]).astype(BF16)
        imag_b = (imag_a * twist[0] - real_a * twist[1]).astype(BF16)
        b = jnp.concatenate([real_b, imag_b], axis=1)
        return jnp.dot(b, ahead[...], preferred_element_type=F32).astype(BF16)

    def arrival(spot, k):
        block = held.at[spot, k]
        pltpu.make_async_copy(block, block, tok_recv.at[spot, k]).wait()

    def forward_copy(d, t):
        k = t * chan + c
        block = held.at[lax.rem(f + d, fsdp), k]
        return pltpu.make_async_remote_copy(
            src_ref=block,
            dst_ref=block,
            send_sem=fwd_send.at[d - 1, t],
            recv_sem=tok_recv.at[lax.rem(f + d, fsdp), k],
            device_id={"chan": sibling},
            device_id_type=MESH,
        )

    def part_copy(d, j):
        return pltpu.make_async_remote_copy(
            src_ref=psend.at[d - 1, j],
            dst_ref=precv.at[d - 1, j],
            send_sem=part_send.at[d - 1, j],
            recv_sem=part_recv.at[d - 1, j],
            device_id={"fsdp": lax.rem(f + d, fsdp)},
            device_id_type=MESH,
        )

    phases = ((1, 2), (0, 1))

    def halo_target(d):
        return s * fsdp + lax.rem(f + d, fsdp) + 1

    def halo_copy(d, phase):
        target = jnp.minimum(halo_target(d), groups - 1)
        start, count = phases[phase]
        return pltpu.make_async_remote_copy(
            src_ref=acc.at[d - 1, pl.ds(start, count), pl.ds(rows - 8, 8)],
            dst_ref=hrecv.at[f, pl.ds(start, count)],
            send_sem=halo_send.at[d - 1, phase],
            recv_sem=halo_recv.at[f, phase],
            device_id={"seq": target // fsdp, "fsdp": target % fsdp},
            device_id_type=MESH,
        )

    def halo_remote(d):
        target = halo_target(d)
        return jnp.logical_and(target < groups, target != me)

    def halo_start(d, phase):
        @pl.when(halo_remote(d))
        def _():
            halo_copy(d, phase).start()

        start, count = phases[phase]

        @pl.when(halo_target(d) == me)
        def _():
            hrecv[f, start : start + count] = acc[d - 1, start : start + count, rows - 8 :]

    def halo_wait(phase):
        start, count = phases[phase]
        for h in range(fsdp):
            local = jnp.logical_and(f > 0, f == h)

            @pl.when(jnp.logical_and(me > 0, jnp.logical_not(local)))
            def _():
                block = hrecv.at[h, pl.ds(start, count)]
                pltpu.make_async_copy(block, block, halo_recv.at[h, phase]).wait()

    @pl.when(me == 0)
    def _():
        hrecv[...] = jnp.zeros_like(hrecv)

    loads[1].wait()
    for k in range(CHUNKS):
        arrival(f, k)
        for j in (1, 2):
            term = jnp.dot(held[f, k], w[j, k], preferred_element_type=F32)
            acc[fsdp - 1, j] = term if k == 0 else acc[fsdp - 1, j] + term
    halo_start(fsdp, 0)

    for d in range(1, fsdp):
        spot = lax.rem(f + d, fsdp)
        for t in range(CHUNKS // chan):
            for b in range(chan):
                k = t * chan + lax.rem(c + b, chan)
                arrival(spot, k)
                if b == 0:
                    forward_copy(d, t).start()
                final = (t + 1) * chan == CHUNKS and b == chan - 1
                for j in (1, 2):
                    term = jnp.dot(held[spot, k], w[j, k], preferred_element_type=F32)
                    if t > 0 or b > 0:
                        term = acc[d - 1, j] + term
                    acc[d - 1, j] = term
                    if final:
                        psend[d - 1, j] = term.astype(BF16)
                        part_copy(d, j).start()
        halo_start(d, 0)

    for load in loads[2:]:
        load.wait()
    exchange_wait(0, tsend, trecv)
    tapspec[...] = spectrum(trecv[...].reshape(width, rows))

    row_ids = lax.broadcasted_iota(jnp.int32, (rows, width), 0)

    def branch(j):
        total = acc[fsdp - 1, j]
        edge = hrecv[0, j]
        for d in range(1, fsdp):
            part_copy(d, j).wait_recv()
            total = total + precv[d - 1, j].astype(F32)
            edge = edge + hrecv[d, j]
        now = total.astype(BF16).astype(F32)
        edge = edge.astype(BF16).astype(F32)
        before = edge[7:8]
        earlier = edge[6:7]
        one = jnp.where(row_ids == 0, before, pltpu.roll(now, 1, 0))
        two = jnp.where(
            row_ids == 0, earlier, jnp.where(row_ids == 1, before, pltpu.roll(now, 2, 0))
        )
        return (
            short[0, j : j + 1, :] * now
            + short[1, j : j + 1, :] * one
            + short[2, j : j + 1, :] * two
        )

    halo_wait(0)
    prod = (branch(1) * branch(2)).astype(BF16).astype(F32)
    gsend[...] = jnp.transpose(prod).astype(BF16).reshape(groups, per, rows)
    exchange_start(1, gsend, grecv)
    product[...] = prod * gain[...]

    for d in range(1, fsdp + 1):
        spot = lax.rem(f + d, fsdp)
        term = jnp.dot(held[spot, 0], w[0, 0], preferred_element_type=F32)
        for k in range(1, CHUNKS):
            term += jnp.dot(held[spot, k], w[0, k], preferred_element_type=F32)
        acc[d - 1, 0] = term
        if d < fsdp:
            psend[d - 1, 0] = term.astype(BF16)
            part_copy(d, 0).start()
        halo_start(d, 1)

    exchange_wait(1, gsend, grecv)

    x = spectrum(grecv[...].reshape(width, rows)).astype(F32)
    t = tapspec[...].astype(F32)
    xr, xi = x[:, :rows], x[:, rows:]
    tr, ti = t[:, :rows], t[:, rows:]
    real_z = (xr * tr - xi * ti).astype(BF16)
    imag_z = (xr * ti + xi * tr).astype(BF16)
    z = jnp.concatenate([real_z, imag_z], axis=1)
    v = jnp.dot(z, behind[...], preferred_element_type=F32)
    vr, vi = v[:, :rows], v[:, rows:]
    real_w = (vr * twist[0] - vi * twist[1]).astype(BF16)
    imag_w = (vi * twist[0] + vr * twist[1]).astype(BF16)
    packed = jnp.concatenate([real_w, imag_w], axis=0)
    y = jnp.dot(last[...], packed, preferred_element_type=F32) * (1.0 / (bins * rows))
    csend[...] = y.astype(BF16).reshape(groups, per, rows)
    exchange_start(2, csend, crecv)
    halo_wait(1)
    query[...] = branch(0)
    exchange_wait(2, csend, crecv)
    conv = jnp.transpose(crecv[...].reshape(width, rows).astype(F32))
    out[...] = (query[...] * (conv + product[...])).astype(BF16)

    for d in range(1, fsdp + 1):
        for phase in range(2):

            @pl.when(halo_remote(d))
            def _():
                halo_copy(d, phase).wait_send()

    for d in range(1, fsdp):
        for j in range(3):
            part_copy(d, j).wait_send()
        for t in range(CHUNKS // chan):
            forward_copy(d, t).wait_send()
    for k in range(CHUNKS):
        for i in range(share):
            token_copy(i, k, False).wait_send()


def per_device(sizes, tokens, proj_weight, short_weight, skip_gain, filter_taps):
    seq, fsdp, chan = sizes
    groups = seq * fsdp
    rows = tokens.shape[0]
    depth, branches, width = proj_weight.shape
    per = width // groups
    made = tables(groups, per, rows)
    dma = pltpu.SemaphoreType.DMA
    vmem = pl.BlockSpec(memory_space=pltpu.VMEM)
    hbm = pl.BlockSpec(memory_space=pl.ANY)
    half = 2 * groups * per
    return pl.pallas_call(
        functools.partial(kernel, sizes),
        out_shape=jax.ShapeDtypeStruct((rows, width), BF16),
        in_specs=[hbm] * 10,
        out_specs=vmem,
        scratch_shapes=[
            pltpu.VMEM((branches, CHUNKS, depth // CHUNKS, width), BF16),
            pltpu.VMEM(made[0].shape, BF16),
            pltpu.VMEM(made[1].shape, BF16),
            pltpu.VMEM(made[2].shape, BF16),
            pltpu.VMEM(made[3].shape, BF16),
            pltpu.VMEM(made[4].shape, F32),
            pltpu.VMEM(short_weight.shape, F32),
            pltpu.VMEM((1, width), F32),
            pltpu.VMEM((rows, width), BF16),
            pltpu.VMEM((fsdp, CHUNKS, rows, depth // CHUNKS), BF16),
            pltpu.VMEM((fsdp, branches, rows, width), F32),
            pltpu.VMEM((fsdp - 1, branches, rows, width), BF16),
            pltpu.VMEM((fsdp - 1, branches, rows, width), BF16),
            pltpu.VMEM((fsdp, branches, 8, width), F32),
            pltpu.VMEM((rows, width), F32),
            pltpu.VMEM((rows, width), F32),
        ]
        + [pltpu.VMEM((groups, per, rows), BF16)] * 6
        + [
            pltpu.VMEM((half, 2 * rows), BF16),
            dma((10,)),
            dma((fsdp // chan, CHUNKS)),
            dma((fsdp, CHUNKS)),
            dma((fsdp - 1, CHUNKS // chan)),
            dma((fsdp - 1, branches)),
            dma((fsdp - 1, branches)),
            dma((fsdp, 2)),
            dma((fsdp, 2)),
            dma((3, groups)),
            dma((3, groups)),
        ],
        compiler_params=pltpu.CompilerParams(
            collective_id=0, has_side_effects=True, vmem_limit_bytes=60 * 1024 * 1024
        ),
        name="hyena",
    )(
        tokens,
        jnp.transpose(proj_weight, (1, 0, 2)).reshape(branches, CHUNKS, depth // CHUNKS, width),
        short_weight,
        skip_gain.reshape(1, width),
        filter_taps,
        *[jnp.asarray(table) for table in made],
    )


def solution(mesh):
    sizes = (mesh.shape["seq"], mesh.shape["fsdp"], mesh.shape["chan"])
    in_specs = (
        P(("grp", "seq", "fsdp"), "chan"),
        P("fsdp", None, "chan"),
        P(None, None, "chan"),
        P("chan"),
        P(("seq", "fsdp"), "chan"),
    )
    out_specs = P(("grp", "seq", "fsdp"), "chan")
    return jax.shard_map(
        functools.partial(per_device, sizes),
        mesh=mesh,
        in_specs=in_specs,
        out_specs=out_specs,
        check_vma=False,
    )
```

```python
import functools
import math

import jax
import jax.numpy as jnp
import ml_dtypes
import numpy as np
from jax import lax
from jax.experimental import pallas as pl
from jax.experimental.pallas import tpu as pltpu
from jax.sharding import PartitionSpec as P

MESH = pl.DeviceIdType.MESH
BF16 = jnp.bfloat16
F32 = jnp.float32
MOST_CHUNKS = 2
HALVES = 2


def phase_pair(rows, cols, period):
    wrapped = (np.arange(rows)[:, None] * np.arange(cols)[None, :]) % period
    phase = wrapped.astype(np.float32) * np.float32(2.0 * math.pi / period)
    return np.cos(phase), np.sin(phase)


def tables(groups, per, rows):
    bf = ml_dtypes.bfloat16
    bins = 2 * groups
    cos, sin = phase_pair(bins, groups, bins)
    eye = np.eye(per, dtype=np.float32)
    first = np.concatenate([np.kron(cos, eye), np.kron(-sin, eye)], axis=0).astype(bf)
    cos, sin = phase_pair(rows, rows, rows)
    ahead = np.block([[cos, -sin], [sin, cos]]).astype(bf)
    behind = np.block([[cos, sin], [-sin, cos]]).astype(bf)
    cos, sin = phase_pair(bins, rows, bins * rows)
    twist = np.stack([np.repeat(cos, per, axis=0), np.repeat(sin, per, axis=0)])
    last = np.ascontiguousarray(first.T)
    return first, last, ahead, behind, twist.astype(np.float32)


def kernel(
    sizes,
    tokens,
    weight,
    short_h,
    gain_h,
    taps_h,
    first_h,
    last_h,
    ahead_h,
    behind_h,
    twist_h,
    out,
    w,
    first,
    last,
    ahead,
    behind,
    twist,
    short,
    gain,
    taps,
    held,
    acc,
    psend,
    precv,
    hrecv,
    query,
    product,
    tsend,
    trecv,
    gsend,
    grecv,
    csend,
    crecv,
    tapspec,
    load_sem,
    tok_send,
    tok_recv,
    fwd_send,
    part_send,
    part_recv,
    halo_send,
    halo_recv,
    a2a_send,
    a2a_recv,
):
    seq, fsdp, chan = sizes
    groups = seq * fsdp
    rows = tokens.shape[0]
    chunks = weight.shape[1]
    lines = rows // HALVES
    depth = chunks * weight.shape[2]
    width = weight.shape[3]
    per = width // groups
    bins = 2 * groups
    step = depth // chunks
    share = fsdp // chan
    s = lax.axis_index("seq")
    f = lax.axis_index("fsdp")
    c = lax.axis_index("chan")
    me = s * fsdp + f

    loads = [
        pltpu.make_async_copy(source, target, load_sem.at[i])
        for i, (source, target) in enumerate(
            [
                (taps_h, taps),
                (weight.at[pl.ds(1, 2)], w.at[pl.ds(1, 2)]),
                (first_h, first),
                (ahead_h, ahead),
                (twist_h, twist),
                (last_h, last),
                (behind_h, behind),
                (short_h, short),
                (gain_h, gain),
                (weight.at[pl.ds(0, 1)], w.at[pl.ds(0, 1)]),
            ]
        )
    ]
    for load in loads:
        load.start()

    barrier = pltpu.get_barrier_semaphore()
    everyone = groups * chan

    def greet(k, carry):
        other = lax.rem(me * chan + c + k, everyone)
        spot = other // chan
        pl.semaphore_signal(
            barrier,
            inc=1,
            device_id={"seq": spot // fsdp, "fsdp": spot % fsdp, "chan": other % chan},
            device_id_type=MESH,
        )
        return carry

    lax.fori_loop(1, everyone, greet, 0, unroll=everyone <= 16)

    @pl.when(me == 0)
    def _():
        hrecv[...] = jnp.zeros_like(hrecv)

    loads[0].wait()
    tsend[...] = jnp.transpose(taps[...].astype(F32)).astype(BF16).reshape(groups, per, rows)
    pl.semaphore_wait(barrier, everyone - 1)

    sibling = lax.rem(c + 1, chan)

    def span(h):
        return pl.ds(h * lines, lines)

    def token_copy(i, h, k, same):
        return pltpu.make_async_remote_copy(
            src_ref=tokens.at[span(h), pl.ds(i * depth + k * step, step)],
            dst_ref=held.at[f, k, span(h)],
            send_sem=tok_send.at[i, h, k],
            recv_sem=tok_recv.at[f, h, k],
            device_id={"fsdp": c * share + i, "chan": sibling if same else k % chan},
            device_id_type=MESH,
        )

    for h, k in [(h, k) for h in range(HALVES) for k in range(chunks)]:
        for i in range(share):
            stays = c * share + i == f

            @pl.when(jnp.logical_not(stays))
            def _():
                token_copy(i, h, k, False).start()

            @pl.when(stays)
            def _():
                token_copy(i, h, k, True).start()
                pltpu.make_async_copy(
                    tokens.at[span(h), pl.ds(i * depth + k * step, step)],
                    held.at[f, k, span(h)],
                    tok_recv.at[f, h, k],
                ).start()

    def exchange_copy(which, source, target, k):
        other = lax.rem(me + k, groups)
        return pltpu.make_async_remote_copy(
            src_ref=source.at[other],
            dst_ref=target.at[me],
            send_sem=a2a_send.at[which, k],
            recv_sem=a2a_recv.at[which, k],
            device_id={"seq": other // fsdp, "fsdp": other % fsdp},
            device_id_type=MESH,
        )

    def exchange_start(which, source, target):
        def go(k, carry):
            exchange_copy(which, source, target, k).start()
            return carry

        lax.fori_loop(1, groups, go, 0, unroll=groups <= 8)
        target[me] = source[me]

    def exchange_wait(which, source, target):
        def go(k, carry):
            exchange_copy(which, source, target, k).wait_recv()
            return carry

        lax.fori_loop(1, groups, go, 0, unroll=groups <= 8)

    def exchange_sent(which, source, target):
        def go(k, carry):
            exchange_copy(which, source, target, k).wait_send()
            return carry

        lax.fori_loop(1, groups, go, 0)

    exchange_start(0, tsend, trecv)

    half = bins * per

    def spectrum(signal):
        a = jnp.dot(first[...], signal, preferred_element_type=F32)
        real_a, imag_a = a[:half], a[half:]
        real_b = (real_a * twist[0] + imag_a * twist[1]).astype(BF16)
        imag_b = (imag_a * twist[0] - real_a * twist[1]).astype(BF16)
        b = jnp.concatenate([real_b, imag_b], axis=1)
        return jnp.dot(b, ahead[...], preferred_element_type=F32).astype(BF16)

    def arrival(spot, h, k):
        block = held.at[spot, k, span(h)]
        pltpu.make_async_copy(block, block, tok_recv.at[spot, h, k]).wait()

    def forward_copy(d, h, t):
        k = t * chan + c
        block = held.at[lax.rem(f + d, fsdp), k, span(h)]
        return pltpu.make_async_remote_copy(
            src_ref=block,
            dst_ref=block,
            send_sem=fwd_send.at[d - 1, h, t],
            recv_sem=tok_recv.at[lax.rem(f + d, fsdp), h, k],
            device_id={"chan": sibling},
            device_id_type=MESH,
        )

    def part_copy(d, j, h):
        return pltpu.make_async_remote_copy(
            src_ref=psend.at[d - 1, j, span(h)],
            dst_ref=precv.at[d - 1, j, span(h)],
            send_sem=part_send.at[d - 1, j, h],
            recv_sem=part_recv.at[d - 1, j, h],
            device_id={"fsdp": lax.rem(f + d, fsdp)},
            device_id_type=MESH,
        )

    phases = ((1, 2), (0, 1))

    def halo_target(d):
        return s * fsdp + lax.rem(f + d, fsdp) + 1

    def halo_copy(d, phase):
        target = jnp.minimum(halo_target(d), groups - 1)
        start, count = phases[phase]
        return pltpu.make_async_remote_copy(
            src_ref=acc.at[d - 1, pl.ds(start, count), pl.ds(rows - 8, 8)],
            dst_ref=hrecv.at[f, pl.ds(start, count)],
            send_sem=halo_send.at[d - 1, phase],
            recv_sem=halo_recv.at[f, phase],
            device_id={"seq": target // fsdp, "fsdp": target % fsdp},
            device_id_type=MESH,
        )

    def halo_remote(d):
        target = halo_target(d)
        return jnp.logical_and(target < groups, target != me)

    def halo_start(d, phase):
        @pl.when(halo_remote(d))
        def _():
            halo_copy(d, phase).start()

        start, count = phases[phase]

        @pl.when(halo_target(d) == me)
        def _():
            hrecv[f, start : start + count] = acc[d - 1, start : start + count, rows - 8 :]

    def halo_wait(phase):
        start, count = phases[phase]
        for h in range(fsdp):
            local = jnp.logical_and(f > 0, f == h)

            @pl.when(jnp.logical_and(me > 0, jnp.logical_not(local)))
            def _():
                block = hrecv.at[h, pl.ds(start, count)]
                pltpu.make_async_copy(block, block, halo_recv.at[h, phase]).wait()

    loads[1].wait()
    for k in range(chunks):
        for h in range(HALVES):
            arrival(f, h, k)
        for j in (1, 2):
            term = jnp.dot(held[f, k], w[j, k], preferred_element_type=F32)
            acc[fsdp - 1, j] = term if k == 0 else acc[fsdp - 1, j] + term
    halo_start(fsdp, 0)

    for d in range(1, fsdp):
        spot = lax.rem(f + d, fsdp)
        for h, t, b in [
            (h, t, b)
            for h in range(HALVES)
            for t in range(chunks // chan)
            for b in range(chan)
        ]:
            k = t * chan + lax.rem(c + b, chan)
            arrival(spot, h, k)
            if b == 0:
                forward_copy(d, h, t).start()
            final = (t + 1) * chan == chunks and b == chan - 1
            at = slice(h * lines, (h + 1) * lines)
            for j in (1, 2):
                term = jnp.dot(held[spot, k, at], w[j, k], preferred_element_type=F32)
                if t > 0 or b > 0:
                    term = acc[d - 1, j, at] + term
                acc[d - 1, j, at] = term
                if final:
                    psend[d - 1, j, at] = term.astype(BF16)
                    part_copy(d, j, h).start()
        halo_start(d, 0)

    for load in loads[2:]:
        load.wait()
    exchange_wait(0, tsend, trecv)
    tapspec[...] = spectrum(trecv[...].reshape(width, rows))

    row_ids = lax.broadcasted_iota(jnp.int32, (rows, width), 0)

    def branch(j):
        total = acc[fsdp - 1, j]
        edge = hrecv[0, j]
        for d in range(1, fsdp):
            for h in range(HALVES):
                part_copy(d, j, h).wait_recv()
            total = total + precv[d - 1, j].astype(F32)
            edge = edge + hrecv[d, j]
        now = total.astype(BF16).astype(F32)
        edge = edge.astype(BF16).astype(F32)
        before = edge[7:8]
        earlier = edge[6:7]
        one = jnp.where(row_ids == 0, before, pltpu.roll(now, 1, 0))
        two = jnp.where(
            row_ids == 0, earlier, jnp.where(row_ids == 1, before, pltpu.roll(now, 2, 0))
        )
        return (
            short[0, j : j + 1, :] * now
            + short[1, j : j + 1, :] * one
            + short[2, j : j + 1, :] * two
        )

    halo_wait(0)
    prod = (branch(1) * branch(2)).astype(BF16).astype(F32)
    gsend[...] = jnp.transpose(prod).astype(BF16).reshape(groups, per, rows)
    exchange_start(1, gsend, grecv)
    product[...] = prod * gain[...]

    for d in range(1, fsdp + 1):
        spot = lax.rem(f + d, fsdp)
        term = jnp.dot(held[spot, 0], w[0, 0], preferred_element_type=F32)
        for k in range(1, chunks):
            term += jnp.dot(held[spot, k], w[0, k], preferred_element_type=F32)
        acc[d - 1, 0] = term
        if d < fsdp:
            psend[d - 1, 0] = term.astype(BF16)
            for h in range(HALVES):
                part_copy(d, 0, h).start()
        halo_start(d, 1)

    exchange_wait(1, gsend, grecv)

    x = spectrum(grecv[...].reshape(width, rows)).astype(F32)
    t = tapspec[...].astype(F32)
    xr, xi = x[:, :rows], x[:, rows:]
    tr, ti = t[:, :rows], t[:, rows:]
    real_z = (xr * tr - xi * ti).astype(BF16)
    imag_z = (xr * ti + xi * tr).astype(BF16)
    z = jnp.concatenate([real_z, imag_z], axis=1)
    v = jnp.dot(z, behind[...], preferred_element_type=F32)
    vr, vi = v[:, :rows], v[:, rows:]
    real_w = (vr * twist[0] - vi * twist[1]).astype(BF16)
    imag_w = (vi * twist[0] + vr * twist[1]).astype(BF16)
    packed = jnp.concatenate([real_w, imag_w], axis=0)
    y = jnp.dot(last[...], packed, preferred_element_type=F32) * (1.0 / (bins * rows))
    csend[...] = y.astype(BF16).reshape(groups, per, rows)
    exchange_start(2, csend, crecv)
    halo_wait(1)
    query[...] = branch(0)
    exchange_wait(2, csend, crecv)
    conv = jnp.transpose(crecv[...].reshape(width, rows).astype(F32))
    out[...] = (query[...] * (conv + product[...])).astype(BF16)

    exchange_sent(0, tsend, trecv)
    exchange_sent(1, gsend, grecv)
    exchange_sent(2, csend, crecv)
    for d in range(1, fsdp + 1):
        for phase in range(2):

            @pl.when(halo_remote(d))
            def _():
                halo_copy(d, phase).wait_send()

    for d in range(1, fsdp):
        for h in range(HALVES):
            for j in range(3):
                part_copy(d, j, h).wait_send()
            for t in range(chunks // chan):
                forward_copy(d, h, t).wait_send()
    for h, k in [(h, k) for h in range(HALVES) for k in range(chunks)]:
        for i in range(share):
            token_copy(i, h, k, False).wait_send()


def per_device(sizes, tokens, proj_weight, short_weight, skip_gain, filter_taps):
    seq, fsdp, chan = sizes
    groups = seq * fsdp
    rows = tokens.shape[0]
    depth, branches, width = proj_weight.shape
    per = width // groups
    chunks = min(MOST_CHUNKS, depth // 128)
    made = tables(groups, per, rows)
    dma = pltpu.SemaphoreType.DMA
    vmem = pl.BlockSpec(memory_space=pltpu.VMEM)
    hbm = pl.BlockSpec(memory_space=pl.ANY)
    half = 2 * groups * per
    return pl.pallas_call(
        functools.partial(kernel, sizes),
        out_shape=jax.ShapeDtypeStruct((rows, width), BF16),
        in_specs=[hbm] * 10,
        out_specs=vmem,
        scratch_shapes=[
            pltpu.VMEM((branches, chunks, depth // chunks, width), BF16),
            pltpu.VMEM(made[0].shape, BF16),
            pltpu.VMEM(made[1].shape, BF16),
            pltpu.VMEM(made[2].shape, BF16),
            pltpu.VMEM(made[3].shape, BF16),
            pltpu.VMEM(made[4].shape, F32),
            pltpu.VMEM(short_weight.shape, F32),
            pltpu.VMEM((1, width), F32),
            pltpu.VMEM((rows, width), BF16),
            pltpu.VMEM((fsdp, chunks, rows, depth // chunks), BF16),
            pltpu.VMEM((fsdp, branches, rows, width), F32),
            pltpu.VMEM((fsdp - 1, branches, rows, width), BF16),
            pltpu.VMEM((fsdp - 1, branches, rows, width), BF16),
            pltpu.VMEM((fsdp, branches, 8, width), F32),
            pltpu.VMEM((rows, width), F32),
            pltpu.VMEM((rows, width), F32),
        ]
        + [pltpu.VMEM((groups, per, rows), BF16)] * 6
        + [
            pltpu.VMEM((half, 2 * rows), BF16),
            dma((10,)),
            dma((fsdp // chan, HALVES, chunks)),
            dma((fsdp, HALVES, chunks)),
            dma((fsdp - 1, HALVES, chunks // chan)),
            dma((fsdp - 1, branches, HALVES)),
            dma((fsdp - 1, branches, HALVES)),
            dma((fsdp, 2)),
            dma((fsdp, 2)),
            dma((3, groups)),
            dma((3, groups)),
        ],
        compiler_params=pltpu.CompilerParams(
            collective_id=0, has_side_effects=True, vmem_limit_bytes=60 * 1024 * 1024
        ),
        name="hyena",
    )(
        tokens,
        jnp.transpose(proj_weight, (1, 0, 2)).reshape(branches, chunks, depth // chunks, width),
        short_weight,
        skip_gain.reshape(1, width),
        filter_taps,
        *[jnp.asarray(table) for table in made],
    )


def solution(mesh):
    sizes = (mesh.shape["seq"], mesh.shape["fsdp"], mesh.shape["chan"])
    in_specs = (
        P(("grp", "seq", "fsdp"), "chan"),
        P("fsdp", None, "chan"),
        P(None, None, "chan"),
        P("chan"),
        P(("seq", "fsdp"), "chan"),
    )
    out_specs = P(("grp", "seq", "fsdp"), "chan")
    return jax.shard_map(
        functools.partial(per_device, sizes),
        mesh=mesh,
        in_specs=in_specs,
        out_specs=out_specs,
        check_vma=False,
    )
```

```python
import functools
import math

import jax
import jax.numpy as jnp
import ml_dtypes
import numpy as np
from jax import lax
from jax.experimental import pallas as pl
from jax.experimental.pallas import tpu as pltpu
from jax.sharding import PartitionSpec as P

MESH = pl.DeviceIdType.MESH
BF16 = jnp.bfloat16
F32 = jnp.float32
MOST_CHUNKS = 2
HALVES = 2


def phase_pair(rows, cols, period):
    wrapped = (np.arange(rows)[:, None] * np.arange(cols)[None, :]) % period
    phase = wrapped.astype(np.float32) * np.float32(2.0 * math.pi / period)
    return np.cos(phase), np.sin(phase)


def tables(groups, per, rows):
    bf = ml_dtypes.bfloat16
    bins = 2 * groups
    cos, sin = phase_pair(bins, groups, bins)
    eye = np.eye(per, dtype=np.float32)
    first = np.concatenate([np.kron(cos, eye), np.kron(-sin, eye)], axis=0).astype(bf)
    cos, sin = phase_pair(rows, rows, rows)
    ahead = np.block([[cos, -sin], [sin, cos]]).astype(bf)
    behind = np.block([[cos, sin], [-sin, cos]]).astype(bf)
    cos, sin = phase_pair(bins, rows, bins * rows)
    twist = np.stack([np.repeat(cos, per, axis=0), np.repeat(sin, per, axis=0)])
    last = np.ascontiguousarray(first.T)
    return first, last, ahead, behind, twist.astype(np.float32)


def kernel(
    sizes,
    tokens,
    weight,
    short_h,
    gain_h,
    taps_h,
    first_h,
    last_h,
    ahead_h,
    behind_h,
    twist_h,
    out,
    w,
    first,
    last,
    ahead,
    behind,
    twist,
    short,
    gain,
    taps,
    held,
    acc,
    psend,
    precv,
    hrecv,
    query,
    product,
    tsend,
    trecv,
    gsend,
    grecv,
    csend,
    crecv,
    tapspec,
    load_sem,
    tok_send,
    tok_recv,
    fwd_send,
    part_send,
    part_recv,
    halo_send,
    halo_recv,
    a2a_send,
    a2a_recv,
):
    seq, fsdp, chan = sizes
    groups = seq * fsdp
    rows = tokens.shape[0]
    chunks = weight.shape[1]
    lines = rows // HALVES
    depth = chunks * weight.shape[2]
    width = weight.shape[3]
    per = width // groups
    bins = 2 * groups
    step = depth // chunks
    share = fsdp // chan
    s = lax.axis_index("seq")
    f = lax.axis_index("fsdp")
    c = lax.axis_index("chan")
    me = s * fsdp + f

    loads = [
        pltpu.make_async_copy(source, target, load_sem.at[i])
        for i, (source, target) in enumerate(
            [
                (taps_h, taps),
                (weight.at[pl.ds(1, 2)], w.at[pl.ds(1, 2)]),
                (first_h, first),
                (ahead_h, ahead),
                (twist_h, twist),
                (last_h, last),
                (behind_h, behind),
                (short_h, short),
                (gain_h, gain),
                (weight.at[pl.ds(0, 1)], w.at[pl.ds(0, 1)]),
            ]
        )
    ]
    for load in loads:
        load.start()

    barrier = pltpu.get_barrier_semaphore()
    everyone = groups * chan

    def greet(k, carry):
        other = lax.rem(me * chan + c + k, everyone)
        spot = other // chan
        pl.semaphore_signal(
            barrier,
            inc=1,
            device_id={"seq": spot // fsdp, "fsdp": spot % fsdp, "chan": other % chan},
            device_id_type=MESH,
        )
        return carry

    lax.fori_loop(1, everyone, greet, 0, unroll=everyone <= 16)

    @pl.when(me == 0)
    def _():
        hrecv[...] = jnp.zeros_like(hrecv)

    loads[0].wait()
    tsend[...] = jnp.transpose(taps[...].astype(F32)).astype(BF16).reshape(groups, per, rows)
    pl.semaphore_wait(barrier, everyone - 1)

    sibling = lax.rem(c + 1, chan)

    def span(h):
        return pl.ds(h * lines, lines)

    def token_copy(i, h, k, same):
        return pltpu.make_async_remote_copy(
            src_ref=tokens.at[span(h), pl.ds(i * depth + k * step, step)],
            dst_ref=held.at[f, k, span(h)],
            send_sem=tok_send.at[i, h, k],
            recv_sem=tok_recv.at[f, h, k],
            device_id={"fsdp": c * share + i, "chan": sibling if same else k % chan},
            device_id_type=MESH,
        )

    for h, k in [(h, k) for h in range(HALVES) for k in range(chunks)]:
        for i in range(share):
            stays = c * share + i == f

            @pl.when(jnp.logical_not(stays))
            def _():
                token_copy(i, h, k, False).start()

            @pl.when(stays)
            def _():
                token_copy(i, h, k, True).start()
                pltpu.make_async_copy(
                    tokens.at[span(h), pl.ds(i * depth + k * step, step)],
                    held.at[f, k, span(h)],
                    tok_recv.at[f, h, k],
                ).start()

    def exchange_copy(which, source, target, k):
        other = lax.rem(me + k, groups)
        return pltpu.make_async_remote_copy(
            src_ref=source.at[other],
            dst_ref=target.at[me],
            send_sem=a2a_send.at[which, k],
            recv_sem=a2a_recv.at[which, k],
            device_id={"seq": other // fsdp, "fsdp": other % fsdp},
            device_id_type=MESH,
        )

    def exchange_start(which, source, target):
        def go(k, carry):
            exchange_copy(which, source, target, k).start()
            return carry

        lax.fori_loop(1, groups, go, 0, unroll=groups <= 8)
        target[me] = source[me]

    def exchange_wait(which, source, target):
        def go(k, carry):
            exchange_copy(which, source, target, k).wait_recv()
            return carry

        lax.fori_loop(1, groups, go, 0, unroll=groups <= 8)

    def exchange_sent(which, source, target):
        def go(k, carry):
            exchange_copy(which, source, target, k).wait_send()
            return carry

        lax.fori_loop(1, groups, go, 0)


    half = bins * per

    def spectrum(signal):
        a = jnp.dot(first[...], signal, preferred_element_type=F32)
        real_a, imag_a = a[:half], a[half:]
        real_b = (real_a * twist[0] + imag_a * twist[1]).astype(BF16)
        imag_b = (imag_a * twist[0] - real_a * twist[1]).astype(BF16)
        b = jnp.concatenate([real_b, imag_b], axis=1)
        return jnp.dot(b, ahead[...], preferred_element_type=F32).astype(BF16)

    def arrival(spot, h, k):
        block = held.at[spot, k, span(h)]
        pltpu.make_async_copy(block, block, tok_recv.at[spot, h, k]).wait()

    def forward_copy(d, h, t):
        k = t * chan + c
        block = held.at[lax.rem(f + d, fsdp), k, span(h)]
        return pltpu.make_async_remote_copy(
            src_ref=block,
            dst_ref=block,
            send_sem=fwd_send.at[d - 1, h, t],
            recv_sem=tok_recv.at[lax.rem(f + d, fsdp), h, k],
            device_id={"chan": sibling},
            device_id_type=MESH,
        )

    def part_copy(d, j, h):
        return pltpu.make_async_remote_copy(
            src_ref=psend.at[d - 1, j, span(h)],
            dst_ref=precv.at[d - 1, j, span(h)],
            send_sem=part_send.at[d - 1, j, h],
            recv_sem=part_recv.at[d - 1, j, h],
            device_id={"fsdp": lax.rem(f + d, fsdp)},
            device_id_type=MESH,
        )

    phases = ((1, 2), (0, 1))

    def halo_target(d):
        return s * fsdp + lax.rem(f + d, fsdp) + 1

    def halo_copy(d, phase):
        target = jnp.minimum(halo_target(d), groups - 1)
        start, count = phases[phase]
        return pltpu.make_async_remote_copy(
            src_ref=acc.at[d - 1, pl.ds(start, count), pl.ds(rows - 8, 8)],
            dst_ref=hrecv.at[f, pl.ds(start, count)],
            send_sem=halo_send.at[d - 1, phase],
            recv_sem=halo_recv.at[f, phase],
            device_id={"seq": target // fsdp, "fsdp": target % fsdp},
            device_id_type=MESH,
        )

    def halo_remote(d):
        target = halo_target(d)
        return jnp.logical_and(target < groups, target != me)

    def halo_start(d, phase):
        @pl.when(halo_remote(d))
        def _():
            halo_copy(d, phase).start()

        start, count = phases[phase]

        @pl.when(halo_target(d) == me)
        def _():
            hrecv[f, start : start + count] = acc[d - 1, start : start + count, rows - 8 :]

    def halo_wait(phase):
        start, count = phases[phase]
        for h in range(fsdp):
            local = jnp.logical_and(f > 0, f == h)

            @pl.when(jnp.logical_and(me > 0, jnp.logical_not(local)))
            def _():
                block = hrecv.at[h, pl.ds(start, count)]
                pltpu.make_async_copy(block, block, halo_recv.at[h, phase]).wait()

    loads[1].wait()
    for k in range(chunks):
        for h in range(HALVES):
            arrival(f, h, k)
        for j in (1, 2):
            term = jnp.dot(held[f, k], w[j, k], preferred_element_type=F32)
            acc[fsdp - 1, j] = term if k == 0 else acc[fsdp - 1, j] + term
    halo_start(fsdp, 0)

    for d in range(1, fsdp):
        spot = lax.rem(f + d, fsdp)
        for h, t, b in [
            (h, t, b)
            for h in range(HALVES)
            for t in range(chunks // chan)
            for b in range(chan)
        ]:
            k = t * chan + lax.rem(c + b, chan)
            arrival(spot, h, k)
            if b == 0:
                forward_copy(d, h, t).start()
            final = (t + 1) * chan == chunks and b == chan - 1
            at = slice(h * lines, (h + 1) * lines)
            for j in (1, 2):
                term = jnp.dot(held[spot, k, at], w[j, k], preferred_element_type=F32)
                if t > 0 or b > 0:
                    term = acc[d - 1, j, at] + term
                acc[d - 1, j, at] = term
                if final:
                    psend[d - 1, j, at] = term.astype(BF16)
                    part_copy(d, j, h).start()
        halo_start(d, 0)

    for load in loads[2:]:
        load.wait()
    exchange_start(0, tsend, trecv)

    row_ids = lax.broadcasted_iota(jnp.int32, (rows, width), 0)

    def branch(j):
        total = acc[fsdp - 1, j]
        edge = hrecv[0, j]
        for d in range(1, fsdp):
            for h in range(HALVES):
                part_copy(d, j, h).wait_recv()
            total = total + precv[d - 1, j].astype(F32)
            edge = edge + hrecv[d, j]
        now = total.astype(BF16).astype(F32)
        edge = edge.astype(BF16).astype(F32)
        before = edge[7:8]
        earlier = edge[6:7]
        one = jnp.where(row_ids == 0, before, pltpu.roll(now, 1, 0))
        two = jnp.where(
            row_ids == 0, earlier, jnp.where(row_ids == 1, before, pltpu.roll(now, 2, 0))
        )
        return (
            short[0, j : j + 1, :] * now
            + short[1, j : j + 1, :] * one
            + short[2, j : j + 1, :] * two
        )

    halo_wait(0)
    prod = (branch(1) * branch(2)).astype(BF16).astype(F32)
    gsend[...] = jnp.transpose(prod).astype(BF16).reshape(groups, per, rows)
    exchange_start(1, gsend, grecv)
    product[...] = prod * gain[...]

    for d in range(1, fsdp + 1):
        spot = lax.rem(f + d, fsdp)
        term = jnp.dot(held[spot, 0], w[0, 0], preferred_element_type=F32)
        for k in range(1, chunks):
            term += jnp.dot(held[spot, k], w[0, k], preferred_element_type=F32)
        acc[d - 1, 0] = term
        if d < fsdp:
            psend[d - 1, 0] = term.astype(BF16)

    exchange_wait(0, tsend, trecv)
    tapspec[...] = spectrum(trecv[...].reshape(width, rows))
    exchange_wait(1, gsend, grecv)
    for d in range(1, fsdp + 1):
        if d < fsdp:
            for h in range(HALVES):
                part_copy(d, 0, h).start()
        halo_start(d, 1)

    x = spectrum(grecv[...].reshape(width, rows)).astype(F32)
    t = tapspec[...].astype(F32)
    xr, xi = x[:, :rows], x[:, rows:]
    tr, ti = t[:, :rows], t[:, rows:]
    real_z = (xr * tr - xi * ti).astype(BF16)
    imag_z = (xr * ti + xi * tr).astype(BF16)
    z = jnp.concatenate([real_z, imag_z], axis=1)
    v = jnp.dot(z, behind[...], preferred_element_type=F32)
    vr, vi = v[:, :rows], v[:, rows:]
    real_w = (vr * twist[0] - vi * twist[1]).astype(BF16)
    imag_w = (vi * twist[0] + vr * twist[1]).astype(BF16)
    packed = jnp.concatenate([real_w, imag_w], axis=0)
    y = jnp.dot(last[...], packed, preferred_element_type=F32) * (1.0 / (bins * rows))
    csend[...] = y.astype(BF16).reshape(groups, per, rows)
    exchange_start(2, csend, crecv)
    halo_wait(1)
    query[...] = branch(0)
    exchange_wait(2, csend, crecv)
    conv = jnp.transpose(crecv[...].reshape(width, rows).astype(F32))
    out[...] = (query[...] * (conv + product[...])).astype(BF16)

    exchange_sent(0, tsend, trecv)
    exchange_sent(1, gsend, grecv)
    exchange_sent(2, csend, crecv)
    for d in range(1, fsdp + 1):
        for phase in range(2):

            @pl.when(halo_remote(d))
            def _():
                halo_copy(d, phase).wait_send()

    for d in range(1, fsdp):
        for h in range(HALVES):
            for j in range(3):
                part_copy(d, j, h).wait_send()
            for t in range(chunks // chan):
                forward_copy(d, h, t).wait_send()
    for h, k in [(h, k) for h in range(HALVES) for k in range(chunks)]:
        for i in range(share):
            token_copy(i, h, k, False).wait_send()


def per_device(sizes, tokens, proj_weight, short_weight, skip_gain, filter_taps):
    seq, fsdp, chan = sizes
    groups = seq * fsdp
    rows = tokens.shape[0]
    depth, branches, width = proj_weight.shape
    per = width // groups
    chunks = min(MOST_CHUNKS, depth // 128)
    made = tables(groups, per, rows)
    dma = pltpu.SemaphoreType.DMA
    vmem = pl.BlockSpec(memory_space=pltpu.VMEM)
    hbm = pl.BlockSpec(memory_space=pl.ANY)
    half = 2 * groups * per
    return pl.pallas_call(
        functools.partial(kernel, sizes),
        out_shape=jax.ShapeDtypeStruct((rows, width), BF16),
        in_specs=[hbm] * 10,
        out_specs=vmem,
        scratch_shapes=[
            pltpu.VMEM((branches, chunks, depth // chunks, width), BF16),
            pltpu.VMEM(made[0].shape, BF16),
            pltpu.VMEM(made[1].shape, BF16),
            pltpu.VMEM(made[2].shape, BF16),
            pltpu.VMEM(made[3].shape, BF16),
            pltpu.VMEM(made[4].shape, F32),
            pltpu.VMEM(short_weight.shape, F32),
            pltpu.VMEM((1, width), F32),
            pltpu.VMEM((rows, width), BF16),
            pltpu.VMEM((fsdp, chunks, rows, depth // chunks), BF16),
            pltpu.VMEM((fsdp, branches, rows, width), F32),
            pltpu.VMEM((fsdp - 1, branches, rows, width), BF16),
            pltpu.VMEM((fsdp - 1, branches, rows, width), BF16),
            pltpu.VMEM((fsdp, branches, 8, width), F32),
            pltpu.VMEM((rows, width), F32),
            pltpu.VMEM((rows, width), F32),
        ]
        + [pltpu.VMEM((groups, per, rows), BF16)] * 6
        + [
            pltpu.VMEM((half, 2 * rows), BF16),
            dma((10,)),
            dma((fsdp // chan, HALVES, chunks)),
            dma((fsdp, HALVES, chunks)),
            dma((fsdp - 1, HALVES, chunks // chan)),
            dma((fsdp - 1, branches, HALVES)),
            dma((fsdp - 1, branches, HALVES)),
            dma((fsdp, 2)),
            dma((fsdp, 2)),
            dma((3, groups)),
            dma((3, groups)),
        ],
        compiler_params=pltpu.CompilerParams(
            collective_id=0, has_side_effects=True, vmem_limit_bytes=60 * 1024 * 1024
        ),
        name="hyena",
    )(
        tokens,
        jnp.transpose(proj_weight, (1, 0, 2)).reshape(branches, chunks, depth // chunks, width),
        short_weight,
        skip_gain.reshape(1, width),
        filter_taps,
        *[jnp.asarray(table) for table in made],
    )


def solution(mesh):
    sizes = (mesh.shape["seq"], mesh.shape["fsdp"], mesh.shape["chan"])
    in_specs = (
        P(("grp", "seq", "fsdp"), "chan"),
        P("fsdp", None, "chan"),
        P(None, None, "chan"),
        P("chan"),
        P(("seq", "fsdp"), "chan"),
    )
    out_specs = P(("grp", "seq", "fsdp"), "chan")
    return jax.shard_map(
        functools.partial(per_device, sizes),
        mesh=mesh,
        in_specs=in_specs,
        out_specs=out_specs,
        check_vma=False,
    )
```
